32 devices in a mesh: band: 8 (over z, x), lon: 4 (over y, core).
Axes of the slice: x: 2, y: 2, z: 4, core: 2. Of those that a mesh axis runs over, the one named last changes fastest.
Arguments:
- coefficients: bfloat16 [8, 640, 4, 64], P('lon', 'band'), may hold values from -6 to 6
- cycle_length: int32 [64], replicated, may hold values from 20 to 5136, as said below
- row_latitude: int32 [64], replicated, may hold values from 0 to 63, each once
- pair_band: int32 [640], replicated, may hold values from 0 to 7, as said below
- gridpoint_factor: bfloat16 [64, 5632], P('band', 'lon'), may hold values from 0.5 to 2
Outputs:
- grid_values: bfloat16 [8, 64, 5632], P(None, 'band', 'lon')
- tendencies: bfloat16 [8, 640, 4, 64], P('lon', 'band')
The draws below stay inside these ranges and needn't reach their ends.
Inputs may be any that keep to these rules, and one draw needn't show every extreme that they name: `cycle_length`: each entry is 20 + 4 i for a whole number i; some entry equals 5136. `pair_band`: each band owns at most 80 pairs and some band owns exactly that many. `row_latitude`: each latitude appears once.
All inputs are finite; a program needn't handle non-finite values.
Results may differ from the reference program's by a relative error of at most 0.0068.
Values may be sent and summed in bfloat16 or wider, within the bound.
A program may use at most 128 MiB of HBM per device.

```python
import math
import jax
import jax.numpy as jnp
from jax import lax

M = 1280
FIELD_LEVELS = 8
LATITUDE_ROWS = 64
PAIR_SLOTS = 80
SLOT_TOTAL = 640
PTS_DEV = 1408
NPTS = 5632
N_BAND = 8
N_LON = 4


def draw_cycle_length(key, part):
    cycle_steps = jax.random.randint(jax.random.fold_in(key, 11), (LATITUDE_ROWS,), 0, M)
    widest = jax.random.randint(jax.random.fold_in(key, 12), (), 0, LATITUDE_ROWS)
    cycle_steps = cycle_steps.at[widest].set(M - 1)
    return (20 + 4 * cycle_steps).astype(jnp.int32)


def draw_pair_band(key, part):
    shuffled = jax.random.permutation(jax.random.fold_in(key, 21), M // 2)
    relabel = jax.random.permutation(jax.random.fold_in(key, 22), N_BAND)
    return relabel[shuffled % N_BAND].astype(jnp.int32)


def steps_of(stream_key, extent, shards, low, largest):
    loudness, own = 1.0, jax.random.fold_in(stream_key, 6)
    for dim, blocks in shards:
        heights = jnp.exp(jax.random.uniform(jax.random.fold_in(own, dim), (blocks,), jnp.float32, low / len(shards), largest / len(shards)))
        loudness = loudness * jnp.repeat(heights, extent[dim] // blocks).reshape([-1 if axis == dim else 1 for axis in range(len(extent))])
    return loudness


def scatter_about(stream_key, dims, deviation, bound, cuts=(), held_as=jnp.bfloat16):
    loudness = steps_of(stream_key, dims, cuts, -0.22, 0.18) if cuts else 1.0
    values = jax.random.normal(stream_key, dims, jnp.float32) * deviation * loudness
    return jnp.minimum(jnp.maximum(values, -bound), bound).astype(held_as)


def setup_inputs(seed: int = 0) -> dict:
    key_of = jax.random.split(jax.random.key(seed), 6)
    coefficients = scatter_about(key_of[0], (FIELD_LEVELS, SLOT_TOTAL, 4, LATITUDE_ROWS), 1.0, 6.0, ((0, 4), (1, 8)))
    cycle_length = draw_cycle_length(jax.random.fold_in(key_of[5], 71), 0)
    row_latitude = jax.random.permutation(key_of[2], LATITUDE_ROWS).astype(jnp.int32)
    pair_band = draw_pair_band(jax.random.fold_in(key_of[5], 71), 0)
    gridpoint_factor = jnp.clip(jnp.exp(math.log(2.0) - 1.3862944 * jax.random.uniform(key_of[4], (LATITUDE_ROWS, NPTS), jnp.float32) ** steps_of(key_of[4], (LATITUDE_ROWS, NPTS), ((0, 8), (1, 4)), -0.2, 0.2)), 0.5, 2.0).astype(jnp.bfloat16)
    return dict(coefficients=coefficients, cycle_length=cycle_length, row_latitude=row_latitude, pair_band=pair_band, gridpoint_factor=gridpoint_factor)


TWO_PI = 2.0 * math.pi

def slot_maps(pair_band, band_count, slot_count, wave_count):
    pair_count = pair_band.shape[0]
    onehot = (pair_band[:, None] == jnp.arange(band_count, dtype=jnp.int32)[None, :]).astype(jnp.int32)
    before = jnp.cumsum(onehot, axis=0).astype(jnp.int32) - onehot
    position_within_band = lax.optimization_barrier(jnp.sum(before * onehot, axis=1)).astype(jnp.int32)
    slot_of_pair = (pair_band * slot_count + position_within_band).astype(jnp.int32)
    slot_of_wave = jnp.concatenate([slot_of_pair, slot_of_pair[::-1]]).astype(jnp.int32)
    member_of_wave = (jnp.arange(wave_count, dtype=jnp.int32) >= pair_count).astype(jnp.int32)
    pair_of_slot = jnp.full((band_count * slot_count,), -1, jnp.int32).at[slot_of_pair].set(jnp.arange(pair_count, dtype=jnp.int32))
    occupied = pair_of_slot >= 0
    first_wave = jnp.where(occupied, pair_of_slot, 0).astype(jnp.int32)
    wave_of_slot = jnp.stack([first_wave, wave_count - 1 - first_wave], axis=1).astype(jnp.int32)
    return (slot_of_wave, member_of_wave, wave_of_slot, occupied)

def cycle_table(lengths, wave_count, points):
    places = jnp.arange(points, dtype=jnp.int32)
    low_index = jnp.arange(32, dtype=jnp.int32)
    high_index = 32 * jnp.arange(wave_count // 32, dtype=jnp.int32)

    def single_period(length):
        scale = TWO_PI / length.astype(jnp.float32)
        fine = (low_index[:, None] * places[None, :] % length).astype(jnp.float32) * scale
        coarse = (high_index[:, None] * places[None, :] % length).astype(jnp.float32) * scale
        cos_fine, sin_fine = (jnp.cos(fine), jnp.sin(fine))
        cos_coarse, sin_coarse = (jnp.cos(coarse), jnp.sin(coarse))
        cosine = cos_coarse[:, None, :] * cos_fine[None] - sin_coarse[:, None, :] * sin_fine[None]
        sine = sin_coarse[:, None, :] * cos_fine[None] + cos_coarse[:, None, :] * sin_fine[None]
        return jnp.stack([cosine.reshape(wave_count, points), -sine.reshape(wave_count, points)]).astype(jnp.bfloat16)
    return lax.map(single_period, lengths)

def turn_factors(lengths, wave_count, offsets):
    wave_index = jnp.arange(wave_count, dtype=jnp.int32)
    turn_count = offsets[:, None, None] * wave_index[None, None, :] % lengths[None, :, None]
    angles = turn_count.astype(jnp.float32) * (TWO_PI / lengths.astype(jnp.float32))[None, :, None]
    return (jnp.cos(angles), jnp.sin(angles))

def kept_mask(lengths, wave_count):
    wave_index = jnp.arange(wave_count, dtype=jnp.int32)
    return (2 * wave_index[None, :] < lengths[:, None]).astype(jnp.float32)

def weighted(fourier, lengths):
    wave_count = fourier.shape[3]
    wave_index = jnp.arange(wave_count, dtype=jnp.int32)
    doubled = jnp.where(wave_index == 0, 1.0, 2.0).astype(jnp.float32)
    factor = doubled[None, :] * kept_mask(lengths, wave_count) * lax.rsqrt(lengths.astype(jnp.float32))[:, None]
    return fourier.astype(jnp.float32) * factor[None, :, None, :]

def turned(scaled, cosines, sine_values):
    real_part = scaled[:, None, :, 0, :]
    imag_part = scaled[:, None, :, 1, :]
    new_real = real_part * cosines[None] - imag_part * sine_values[None]
    new_imag = real_part * sine_values[None] + imag_part * cosines[None]
    return jnp.stack([new_real, new_imag], axis=3).astype(jnp.bfloat16)

def synthesize(coeffs, tables, lengths, offsets):
    values = jnp.einsum('fdrtm,rtml->frdl', coeffs.astype(jnp.float32), tables.astype(jnp.float32))
    places = offsets[None, :, None] + jnp.arange(tables.shape[3], dtype=jnp.int32)[None, None, :]
    inside = places < lengths[:, None, None]
    return jnp.where(inside[None], values, 0.0).astype(jnp.bfloat16)

def analyze(values, tables):
    return jnp.einsum('frdl,rtml->fdrtm', values.astype(jnp.float32), tables.astype(jnp.float32))

def untwist(partials, cosines, sine_values):
    real_part = partials[:, :, :, 0, :]
    imag_part = partials[:, :, :, 1, :]
    new_real = lax.optimization_barrier(jnp.sum(real_part * cosines[None] + imag_part * sine_values[None], axis=1))
    new_imag = lax.optimization_barrier(jnp.sum(imag_part * cosines[None] - real_part * sine_values[None], axis=1))
    return jnp.stack([new_real, new_imag], axis=2)

def finish(summed, lengths):
    wave_count = summed.shape[3]
    factor = kept_mask(lengths, wave_count) * lax.rsqrt(lengths.astype(jnp.float32))[:, None]
    return (summed * factor[None, :, None, :]).astype(jnp.bfloat16)

def reference(coefficients, cycle_length, row_latitude, pair_band, gridpoint_factor):
    slot_of_wave, member_of_wave, wave_of_slot, occupied = slot_maps(pair_band, N_BAND, PAIR_SLOTS, M)
    split_view = coefficients.reshape(FIELD_LEVELS, N_BAND * PAIR_SLOTS, 2, 2, LATITUDE_ROWS)
    picked = split_view[:, slot_of_wave, member_of_wave]
    offsets = (PTS_DEV * jnp.arange(N_LON, dtype=jnp.int32)).astype(jnp.int32)

    def one_row(row_number):
        latitude_value = row_latitude[row_number]
        lengths = jnp.take(cycle_length, latitude_value[None])
        fourier = jnp.transpose(jnp.take(picked, latitude_value[None], axis=3), (0, 3, 2, 1))
        tables = cycle_table(lengths, M, PTS_DEV)
        cosines, sine_values = turn_factors(lengths, M, offsets)
        coeffs = turned(weighted(fourier, lengths), cosines, sine_values)
        blocks = synthesize(coeffs, tables, lengths, offsets)
        factor_row = lax.dynamic_slice_in_dim(gridpoint_factor, row_number, 1, 0)
        products = (factor_row.astype(jnp.float32).reshape(1, 1, N_LON, PTS_DEV) * blocks.astype(jnp.float32)).astype(jnp.bfloat16)
        summed = untwist(analyze(products, tables), cosines, sine_values)
        return (blocks.reshape(FIELD_LEVELS, NPTS), finish(summed, lengths)[:, 0])
    grid_rows, spectral_rows = lax.map(one_row, jnp.arange(LATITUDE_ROWS, dtype=jnp.int32))
    grid_values = jnp.transpose(grid_rows, (1, 0, 2))
    inverse_rows = jnp.zeros((LATITUDE_ROWS,), jnp.int32).at[row_latitude].set(jnp.arange(LATITUDE_ROWS, dtype=jnp.int32))
    by_latitude = jnp.transpose(jnp.take(spectral_rows, inverse_rows, axis=0), (1, 3, 2, 0))
    placed = by_latitude[:, wave_of_slot]
    placed = jnp.where(occupied[None, :, None, None, None], placed, jnp.zeros_like(placed))
    tendencies = placed.reshape(FIELD_LEVELS, N_BAND * PAIR_SLOTS, 4, LATITUDE_ROWS)
    return (grid_values, tendencies)
```

```python
import functools
import math

import jax
import jax.numpy as jnp
import numpy as np
from jax import lax
from jax.experimental import pallas as pl
from jax.experimental.pallas import tpu as pltpu
from jax.sharding import PartitionSpec as P

TWO_PI = 2.0 * math.pi
LANES = 128
CHUNK = 256
AXES = ("band", "lon")


def cos_sin(product, length, inverse):
    turns = jnp.floor(product * inverse + 0.5)
    half = (product - turns * length) * (inverse * (0.5 * TWO_PI))
    square = half * half
    sine = jnp.full_like(half, -1.0 / math.factorial(11))
    for order in (9, 7, 5, 3, 1):
        sine = sine * square + (-1.0) ** (order // 2) / math.factorial(order)
    sine = sine * half
    cosine = jnp.full_like(half, 1.0 / math.factorial(12))
    for order in (10, 8, 6, 4, 2, 0):
        cosine = cosine * square + (-1.0) ** (order // 2) / math.factorial(order)
    return 1.0 - 2.0 * sine * sine, 2.0 * sine * cosine


def row_kernel(
    slot_count,
    length_ref,
    wave_band_ref,
    pair_band_ref,
    spec_ref,
    factor_ref,
    grid_ref,
    out_ref,
    hot,
    lhs,
    total,
    cos_state,
    sin_state,
    cos_step,
    sin_step,
    cos_high,
    sin_high,
    cos_high_step,
    sin_high_step,
):
    row = pl.program_id(0)
    fields = spec_ref.shape[2]
    slots, waves = hot.shape
    pairs = pair_band_ref.shape[0]
    high = waves // LANES

    @pl.when(row == 0)
    def _():
        wave = lax.broadcasted_iota(jnp.int32, (1, waves), 1)
        pair_of_wave = jnp.minimum(wave, waves - 1 - wave)
        wave_band = wave_band_ref[...]
        before = jnp.zeros((1, waves), jnp.int32)
        for start in range(0, pairs, 128):
            size = min(128, pairs - start)
            pair = lax.broadcasted_iota(jnp.int32, (size, waves), 0) + start
            same = (pair_band_ref[start : start + size, :] == wave_band) & (pair < pair_of_wave)
            before = before + jnp.sum(same.astype(jnp.int32), axis=0, keepdims=True)
        slot_of_wave = wave_band * slot_count + before
        for start in range(0, slots, 32):
            slot = lax.broadcasted_iota(jnp.int32, (32, waves), 0) + start
            hot[start : start + 32, :] = jnp.where(slot == slot_of_wave, 1.0, 0.0).astype(
                jnp.bfloat16
            )

    n = length_ref[row]
    length = jnp.full((1, 1), n, jnp.int32).astype(jnp.float32)
    inverse = 1.0 / length
    norm = lax.rsqrt(length)

    wave = lax.broadcasted_iota(jnp.int32, (1, waves), 1)
    kept = jnp.where(2 * wave < n, 1.0, 0.0)
    weight = kept * jnp.where(wave == 0, 1.0, 2.0)
    half = waves // 2
    for t in range(2):
        pieces = []
        for member in range(2):
            pieces.append(
                jnp.dot(
                    spec_ref[0, 2 * member + t],
                    hot[:, member * half : (member + 1) * half],
                    preferred_element_type=jnp.float32,
                )
            )
        ordered = (jnp.concatenate(pieces, axis=1) * weight).astype(jnp.bfloat16)
        for b in range(high):
            part = ordered[:, b * LANES : (b + 1) * LANES]
            if t == 0:
                lhs[b * fields : (b + 1) * fields, 0:LANES] = part
                lhs[(high + b) * fields : (high + b + 1) * fields, LANES : 2 * LANES] = -part
            else:
                lhs[b * fields : (b + 1) * fields, LANES : 2 * LANES] = part
                lhs[(high + b) * fields : (high + b + 1) * fields, 0:LANES] = part

    low_wave = lax.broadcasted_iota(jnp.int32, (LANES, CHUNK), 0).astype(jnp.float32)
    place = lax.broadcasted_iota(jnp.int32, (LANES, CHUNK), 1).astype(jnp.float32)
    cos_state[...], sin_state[...] = cos_sin(low_wave * place, length, inverse)
    step_wave = lax.broadcasted_iota(jnp.int32, (LANES, LANES), 0).astype(jnp.float32)
    cos_step[...], sin_step[...] = cos_sin(step_wave * float(CHUNK), length, inverse)
    padded = cos_high.shape[0]
    high_wave = LANES * lax.broadcasted_iota(jnp.int32, (padded, CHUNK), 0)
    high_place = lax.broadcasted_iota(jnp.int32, (padded, CHUNK), 1)
    cos_high[...], sin_high[...] = cos_sin(
        (high_wave * high_place).astype(jnp.float32), length, inverse
    )
    cos_high_step[...], sin_high_step[...] = cos_sin(
        (high_wave * CHUNK).astype(jnp.float32), length, inverse
    )
    total[...] = jnp.zeros_like(total)
    grid_ref[...] = jnp.zeros_like(grid_ref)

    def chunk(h, carry):
        columns = pl.ds(pl.multiple_of(h * CHUNK, CHUNK), CHUNK)
        cosine, sine = cos_state[...], sin_state[...]
        table = jnp.concatenate([cosine, -sine], axis=0).astype(jnp.bfloat16)
        found = jnp.dot(lhs[...], table, preferred_element_type=jnp.float32)
        high_cos, high_sin = cos_high[...], sin_high[...]
        value = jnp.zeros((fields, CHUNK), jnp.float32)
        for b in range(high):
            real = found[b * fields : (b + 1) * fields]
            imag = found[(high + b) * fields : (high + b + 1) * fields]
            value = value + (real * high_cos[b : b + 1] - imag * high_sin[b : b + 1])
        at = h * CHUNK + lax.broadcasted_iota(jnp.int32, (1, CHUNK), 1)
        value = jnp.where(at < n, value * norm, 0.0).astype(jnp.bfloat16)
        grid_ref[0, :, columns] = value
        product = factor_ref[0, :, columns].astype(jnp.float32) * value.astype(jnp.float32)
        product = product.astype(jnp.bfloat16).astype(jnp.float32)
        turned = [product * high_cos[b : b + 1] for b in range(high)]
        turned += [product * (-high_sin[b : b + 1]) for b in range(high)]
        turned = jnp.concatenate(turned, axis=0).astype(jnp.bfloat16)
        total[...] += lax.dot_general(
            turned, table, (((1,), (1,)), ((), ())), preferred_element_type=jnp.float32
        )
        step_cos = jnp.concatenate([cos_step[...]] * (CHUNK // LANES), axis=1)
        step_sin = jnp.concatenate([sin_step[...]] * (CHUNK // LANES), axis=1)
        cos_state[...] = cosine * step_cos - sine * step_sin
        sin_state[...] = sine * step_cos + cosine * step_sin
        high_step_cos, high_step_sin = cos_high_step[...], sin_high_step[...]
        cos_high[...] = high_cos * high_step_cos - high_sin * high_step_sin
        sin_high[...] = high_sin * high_step_cos + high_cos * high_step_sin
        return carry

    lax.fori_loop(0, (n + CHUNK - 1) // CHUNK, chunk, 0)

    scale = kept * norm
    for t in range(2):
        pieces = []
        for b in range(high):
            real = slice(b * fields, (b + 1) * fields)
            imag = slice((high + b) * fields, (high + b + 1) * fields)
            if t == 0:
                pieces.append(total[real, 0:LANES] - total[imag, LANES : 2 * LANES])
            else:
                pieces.append(total[imag, 0:LANES] + total[real, LANES : 2 * LANES])
        finished = (jnp.concatenate(pieces, axis=1) * scale).astype(jnp.bfloat16)
        for member in range(2):
            out_ref[0, 2 * member + t] = lax.dot_general(
                finished[:, member * half : (member + 1) * half],
                hot[:, member * half : (member + 1) * half],
                (((1,), (1,)), ((), ())),
                preferred_element_type=jnp.float32,
            ).astype(jnp.bfloat16)


def transform_rows(lengths, pair_band, spec, factor, slot_count):
    rows, _, fields, slots = spec.shape
    points = factor.shape[2]
    pairs = pair_band.shape[0]
    waves = 2 * pairs
    high = waves // LANES
    padded = -(-high // 8) * 8
    stacked = 2 * high * fields
    wave_band = jnp.concatenate([pair_band, pair_band[::-1]])[None, :]
    grid_spec = pltpu.PrefetchScalarGridSpec(
        num_scalar_prefetch=1,
        grid=(rows,),
        in_specs=[
            pl.BlockSpec((1, waves), lambda i, *_: (0, 0)),
            pl.BlockSpec((pairs, 1), lambda i, *_: (0, 0)),
            pl.BlockSpec((1, 4, fields, slots), lambda i, *_: (i, 0, 0, 0)),
            pl.BlockSpec((1, 1, points), lambda i, *_: (i, 0, 0)),
        ],
        out_specs=[
            pl.BlockSpec((1, fields, points), lambda i, *_: (i, 0, 0)),
            pl.BlockSpec((1, 4, fields, slots), lambda i, *_: (i, 0, 0, 0)),
        ],
        scratch_shapes=[
            pltpu.VMEM((slots, waves), jnp.bfloat16),
            pltpu.VMEM((stacked, 2 * LANES), jnp.bfloat16),
            pltpu.VMEM((stacked, 2 * LANES), jnp.float32),
            pltpu.VMEM((LANES, CHUNK), jnp.float32),
            pltpu.VMEM((LANES, CHUNK), jnp.float32),
            pltpu.VMEM((LANES, LANES), jnp.float32),
            pltpu.VMEM((LANES, LANES), jnp.float32),
            pltpu.VMEM((padded, CHUNK), jnp.float32),
            pltpu.VMEM((padded, CHUNK), jnp.float32),
            pltpu.VMEM((padded, CHUNK), jnp.float32),
            pltpu.VMEM((padded, CHUNK), jnp.float32),
        ],
    )
    return pl.pallas_call(
        functools.partial(row_kernel, slot_count),
        grid_spec=grid_spec,
        out_shape=[
            jax.ShapeDtypeStruct((rows, fields, points), jnp.bfloat16),
            jax.ShapeDtypeStruct((rows, 4, fields, slots), jnp.bfloat16),
        ],
        compiler_params=pltpu.CompilerParams(dimension_semantics=("arbitrary",)),
    )(lengths, wave_band, pair_band[:, None], spec, factor)


def on_device(coefficients, cycle_length, row_latitude, pair_band, gridpoint_factor):
    bands, lanes = lax.axis_size("band"), lax.axis_size("lon")
    device = lax.axis_index("band") * lanes + lax.axis_index("lon")
    own_fields, slot_count, parts, latitudes = coefficients.shape
    band_rows, points = gridpoint_factor.shape
    fields = own_fields * lanes
    own_rows = -(-band_rows // lanes)
    lane_rows = np.arange(lanes * own_rows)
    inside = np.tile(lane_rows < band_rows, bands)
    clamped = np.minimum(lane_rows, band_rows - 1)
    row_ids = (np.arange(bands)[:, None] * band_rows + clamped[None, :]).reshape(-1)
    held = row_latitude if inside.all() else jnp.take(row_latitude, row_ids)
    onehot = held[:, None] == jnp.arange(latitudes, dtype=jnp.int32)[None, :]
    own = lax.dynamic_slice_in_dim(held, device * own_rows, own_rows)
    lengths = jnp.take(cycle_length, own)

    leaving = jnp.einsum(
        "rl,fstl->rtfs",
        onehot.astype(jnp.bfloat16),
        coefficients,
        preferred_element_type=jnp.float32,
    ).astype(jnp.bfloat16)
    arrived = lax.all_to_all(leaving, AXES, split_axis=0, concat_axis=0, tiled=True)
    arrived = arrived.reshape(bands, lanes, own_rows, parts, own_fields, slot_count)
    spec = jnp.transpose(arrived, (2, 3, 1, 4, 0, 5)).reshape(
        own_rows, parts, fields, bands * slot_count
    )
    factor = gridpoint_factor if inside.all() else jnp.take(gridpoint_factor, clamped, axis=0)
    factor = lax.all_to_all(factor, "lon", split_axis=0, concat_axis=1, tiled=True)

    grid, result = transform_rows(lengths, pair_band, spec, factor[:, None, :], slot_count)

    grid_rows = lax.all_to_all(grid, "lon", split_axis=2, concat_axis=0, tiled=True)
    grid_rows = jnp.transpose(grid_rows, (1, 0, 2))[:, :band_rows]

    result = result.reshape(own_rows, parts, lanes, own_fields, bands, slot_count)
    result = jnp.transpose(result, (4, 2, 0, 1, 3, 5)).reshape(
        bands * lanes * own_rows, parts, own_fields, slot_count
    )
    returned = lax.all_to_all(result, AXES, split_axis=0, concat_axis=0, tiled=True)
    back = onehot & inside[:, None]
    tendencies = jnp.einsum(
        "rtfs,rl->fstl",
        returned,
        back.astype(jnp.bfloat16),
        preferred_element_type=jnp.float32,
    ).astype(jnp.bfloat16)
    return (grid_rows, tendencies)


def solution(mesh):
    return jax.shard_map(
        on_device,
        mesh=mesh,
        in_specs=(P("lon", "band", None, None), P(), P(), P(), P("band", "lon")),
        out_specs=(P(None, "band", "lon"), P("lon", "band", None, None)),
        check_vma=False,
    )
```

```python
import functools
import math

import jax
import jax.numpy as jnp
import numpy as np
from jax import lax
from jax.experimental import pallas as pl
from jax.experimental.pallas import tpu as pltpu
from jax.sharding import PartitionSpec as P

TWO_PI = 2.0 * math.pi
LANES = 128
CHUNK = 256


def cos_sin(product, length, inverse):
    turns = jnp.floor(product * inverse + 0.5)
    half = (product - turns * length) * (inverse * (0.5 * TWO_PI))
    square = half * half
    sine = jnp.full_like(half, -1.0 / math.factorial(11))
    for order in (9, 7, 5, 3, 1):
        sine = sine * square + (-1.0) ** (order // 2) / math.factorial(order)
    sine = sine * half
    cosine = jnp.full_like(half, 1.0 / math.factorial(12))
    for order in (10, 8, 6, 4, 2, 0):
        cosine = cosine * square + (-1.0) ** (order // 2) / math.factorial(order)
    return 1.0 - 2.0 * sine * sine, 2.0 * sine * cosine


MESH = pl.DeviceIdType.MESH


def greet(devices, lanes, me):
    barrier = pltpu.get_barrier_semaphore()

    def signal(k, carry):
        flat = lax.rem(me + k, devices)
        peer = {"band": flat // lanes, "lon": lax.rem(flat, lanes)}
        pl.semaphore_signal(barrier, inc=1, device_id=peer, device_id_type=MESH)
        return carry

    lax.fori_loop(1, devices, signal, 0)
    pl.semaphore_wait(barrier, devices - 1)


def send_chunks(devices, lanes, me, source, target, send_sem, recv_sem):
    def send(k, carry):
        flat = lax.rem(me + k, devices)
        pltpu.make_async_remote_copy(
            src_ref=source.at[flat],
            dst_ref=target.at[me],
            send_sem=send_sem,
            recv_sem=recv_sem,
            device_id={"band": flat // lanes, "lon": lax.rem(flat, lanes)},
            device_id_type=MESH,
        ).start()
        return carry

    lax.fori_loop(1, devices, send, 0)
    target[me] = source[me]


def wait_chunks(devices, lanes, source, target, send_sem, recv_sem):
    pltpu.make_async_remote_copy(
        src_ref=source.at[pl.ds(0, devices - 1)],
        dst_ref=target.at[pl.ds(0, devices - 1)],
        send_sem=send_sem,
        recv_sem=recv_sem,
        device_id={"band": lax.axis_index("band"), "lon": lax.axis_index("lon")},
        device_id_type=MESH,
    ).wait()


def gather_kernel(
    bands, lanes, leaving, factor, arrived, cycles, send_sem, recv_sem, row_send_sem, row_recv_sem
):
    lane = lax.axis_index("lon")
    me = lax.axis_index("band") * lanes + lane
    devices = bands * lanes
    points = factor.shape[1]
    greet(devices, lanes, me)
    copies = []
    for j in range(1, lanes):
        own = pl.ds(pl.multiple_of(lane * points, LANES), points)
        copies.append(
            pltpu.make_async_remote_copy(
                src_ref=factor,
                dst_ref=cycles.at[:, own],
                send_sem=row_send_sem.at[j],
                recv_sem=row_recv_sem.at[j],
                device_id={"lon": lax.rem(lane + j, lanes)},
                device_id_type=MESH,
            )
        )
        copies[-1].start()
    send_chunks(devices, lanes, me, leaving, arrived, send_sem, recv_sem)
    cycles[:, pl.ds(pl.multiple_of(lane * points, LANES), points)] = factor[...]
    for copy in copies:
        copy.wait()
    wait_chunks(devices, lanes, leaving, arrived, send_sem, recv_sem)


def scatter_kernel(
    bands, lanes, grid, leaving, blocks, arrived, send_sem, recv_sem, row_send_sem, row_recv_sem
):
    lane = lax.axis_index("lon")
    me = lax.axis_index("band") * lanes + lane
    devices = bands * lanes
    points = grid.shape[2] // lanes
    greet(devices, lanes, me)
    copies = []
    for j in range(1, lanes):
        other = lax.rem(lane + j, lanes)
        copies.append(
            pltpu.make_async_remote_copy(
                src_ref=grid.at[:, :, pl.ds(pl.multiple_of(other * points, LANES), points)],
                dst_ref=blocks.at[lane],
                send_sem=row_send_sem.at[j],
                recv_sem=row_recv_sem.at[j],
                device_id={"lon": other},
                device_id_type=MESH,
            )
        )
        copies[-1].start()
    send_chunks(devices, lanes, me, leaving, arrived, send_sem, recv_sem)
    blocks[lane] = grid[:, :, pl.ds(pl.multiple_of(lane * points, LANES), points)]
    for copy in copies:
        copy.wait()
    wait_chunks(devices, lanes, leaving, arrived, send_sem, recv_sem)


def exchange(kernel, bands, lanes, collective_id, out_shape, first, second):
    return pl.pallas_call(
        functools.partial(kernel, bands, lanes),
        out_shape=out_shape,
        in_specs=[pl.BlockSpec(memory_space=pltpu.VMEM)] * 2,
        out_specs=[pl.BlockSpec(memory_space=pltpu.VMEM)] * 2,
        scratch_shapes=[
            pltpu.SemaphoreType.DMA,
            pltpu.SemaphoreType.DMA,
            pltpu.SemaphoreType.DMA((lanes,)),
            pltpu.SemaphoreType.DMA((lanes,)),
        ],
        compiler_params=pltpu.CompilerParams(collective_id=collective_id, has_side_effects=True),
    )(first, second)


def row_kernel(
    lanes,
    band_rows,
    order_ref,
    scalars_ref,
    wave_band_ref,
    pair_band_ref,
    arrived_ref,
    factor_ref,
    grid_ref,
    out_ref,
    hot,
    ordered,
    finished,
    lhs,
    total,
    row_factor,
    cos_state,
    sin_state,
    cos_step,
    sin_step,
    cos_high,
    sin_high,
    cos_high_step,
    sin_high_step,
):
    rows, fields = grid_ref.shape[0], grid_ref.shape[1]
    slots, waves = hot.shape
    devices = arrived_ref.shape[0]
    bands = devices // lanes
    pairs = pair_band_ref.shape[0]
    high = waves // LANES
    half = waves // 2
    stacked = arrived_ref.shape[1] * lanes

    wave = lax.broadcasted_iota(jnp.int32, (1, waves), 1)
    pair_of_wave = jnp.minimum(wave, waves - 1 - wave)
    wave_band = wave_band_ref[...]
    before = jnp.zeros((1, waves), jnp.int32)
    for start in range(0, pairs, 128):
        size = min(128, pairs - start)
        pair = lax.broadcasted_iota(jnp.int32, (size, waves), 0) + start
        same = (pair_band_ref[start : start + size, :] == wave_band) & (pair < pair_of_wave)
        before = before + jnp.sum(same.astype(jnp.int32), axis=0, keepdims=True)
    slot_of_wave = wave_band * LANES + before

    def fill(step, carry):
        start = pl.multiple_of(step * 32, 32)
        slot = lax.broadcasted_iota(jnp.int32, (32, waves), 0) + start
        hot[pl.ds(start, 32), :] = jnp.where(slot == slot_of_wave, 1.0, 0.0).astype(jnp.bfloat16)
        return carry

    lax.fori_loop(0, slots // 32, fill, 0)

    pieces = []
    for b in range(bands):
        piece = arrived_ref[b * lanes : (b + 1) * lanes].astype(jnp.float32)
        pieces.append(piece.reshape(stacked, LANES).astype(jnp.bfloat16))
    by_part = jnp.dot(
        order_ref[...], jnp.concatenate(pieces, axis=1), preferred_element_type=jnp.float32
    ).astype(jnp.bfloat16)
    for member in range(2):
        columns = slice(member * half, (member + 1) * half)
        ordered[:, columns] = jnp.dot(
            by_part[member * stacked // 2 : (member + 1) * stacked // 2],
            hot[:, columns],
            preferred_element_type=jnp.float32,
        )

    def one_row(i, carry):
        n = scalars_ref[i]
        row = scalars_ref[rows + i]
        length = jnp.full((1, 1), n, jnp.int32).astype(jnp.float32)
        inverse = 1.0 / length
        norm = lax.rsqrt(length)
        kept = jnp.where(2 * wave < n, 1.0, 0.0)
        weight = kept * jnp.where(wave == 0, 1.0, 2.0)
        chosen = lax.broadcasted_iota(jnp.int32, (band_rows, 1), 0) == row
        row_factor[...] = jnp.sum(
            jnp.where(chosen, factor_ref[...].astype(jnp.float32), 0.0), axis=0, keepdims=True
        )
        for t in range(2):
            own = pl.ds(pl.multiple_of((t * rows + i) * fields, fields), fields)
            weighted = (ordered[own, :] * weight).astype(jnp.bfloat16)
            for b in range(high):
                part = weighted[:, b * LANES : (b + 1) * LANES]
                if t == 0:
                    lhs[b * fields : (b + 1) * fields, 0:LANES] = part
                    lhs[(high + b) * fields : (high + b + 1) * fields, LANES : 2 * LANES] = -part
                else:
                    lhs[b * fields : (b + 1) * fields, LANES : 2 * LANES] = part
                    lhs[(high + b) * fields : (high + b + 1) * fields, 0:LANES] = part

        low_wave = lax.broadcasted_iota(jnp.int32, (LANES, CHUNK), 0).astype(jnp.float32)
        place = lax.broadcasted_iota(jnp.int32, (LANES, CHUNK), 1).astype(jnp.float32)
        cos_state[...], sin_state[...] = cos_sin(low_wave * place, length, inverse)
        step_wave = lax.broadcasted_iota(jnp.int32, (LANES, LANES), 0).astype(jnp.float32)
        cos_step[...], sin_step[...] = cos_sin(step_wave * float(CHUNK), length, inverse)
        padded = cos_high.shape[0]
        high_wave = LANES * lax.broadcasted_iota(jnp.int32, (padded, CHUNK), 0)
        high_place = lax.broadcasted_iota(jnp.int32, (padded, CHUNK), 1)
        cos_high[...], sin_high[...] = cos_sin(
            (high_wave * high_place).astype(jnp.float32), length, inverse
        )
        cos_high_step[...], sin_high_step[...] = cos_sin(
            (high_wave * CHUNK).astype(jnp.float32), length, inverse
        )
        total[...] = jnp.zeros_like(total)
        grid_ref[i] = jnp.zeros(grid_ref.shape[1:], grid_ref.dtype)

        def chunk(h, carry):
            columns = pl.ds(pl.multiple_of(h * CHUNK, CHUNK), CHUNK)
            cosine, sine = cos_state[...], sin_state[...]
            table = jnp.concatenate([cosine, -sine], axis=0).astype(jnp.bfloat16)
            found = jnp.dot(lhs[...], table, preferred_element_type=jnp.float32)
            high_cos, high_sin = cos_high[...], sin_high[...]
            value = jnp.zeros((fields, CHUNK), jnp.float32)
            for b in range(high):
                real = found[b * fields : (b + 1) * fields]
                imag = found[(high + b) * fields : (high + b + 1) * fields]
                value = value + (real * high_cos[b : b + 1] - imag * high_sin[b : b + 1])
            at = h * CHUNK + lax.broadcasted_iota(jnp.int32, (1, CHUNK), 1)
            value = jnp.where(at < n, value * norm, 0.0).astype(jnp.bfloat16)
            grid_ref[i, :, columns] = value
            product = row_factor[:, columns] * value.astype(jnp.float32)
            product = product.astype(jnp.bfloat16).astype(jnp.float32)
            turned = [product * high_cos[b : b + 1] for b in range(high)]
            turned += [product * (-high_sin[b : b + 1]) for b in range(high)]
            turned = jnp.concatenate(turned, axis=0).astype(jnp.bfloat16)
            total[...] += lax.dot_general(
                turned, table, (((1,), (1,)), ((), ())), preferred_element_type=jnp.float32
            )
            step_cos = jnp.concatenate([cos_step[...]] * (CHUNK // LANES), axis=1)
            step_sin = jnp.concatenate([sin_step[...]] * (CHUNK // LANES), axis=1)
            cos_state[...] = cosine * step_cos - sine * step_sin
            sin_state[...] = sine * step_cos + cosine * step_sin
            high_step_cos, high_step_sin = cos_high_step[...], sin_high_step[...]
            cos_high[...] = high_cos * high_step_cos - high_sin * high_step_sin
            sin_high[...] = high_sin * high_step_cos + high_cos * high_step_sin
            return carry

        lax.fori_loop(0, (n + CHUNK - 1) // CHUNK, chunk, 0)

        scale = kept * norm
        for t in range(2):
            pieces = []
            for b in range(high):
                real = slice(b * fields, (b + 1) * fields)
                imag = slice((high + b) * fields, (high + b + 1) * fields)
                if t == 0:
                    pieces.append(total[real, 0:LANES] - total[imag, LANES : 2 * LANES])
                else:
                    pieces.append(total[imag, 0:LANES] + total[real, LANES : 2 * LANES])
            own = pl.ds(pl.multiple_of((t * rows + i) * fields, fields), fields)
            finished[own, :] = jnp.concatenate(pieces, axis=1) * scale
        return carry

    lax.fori_loop(0, rows, one_row, 0)

    pieces = []
    for member in range(2):
        columns = slice(member * half, (member + 1) * half)
        pieces.append(
            lax.dot_general(
                finished[:, columns].astype(jnp.bfloat16),
                hot[:, columns],
                (((1,), (1,)), ((), ())),
                preferred_element_type=jnp.float32,
            )
        )
    by_part = jnp.concatenate(pieces, axis=0).astype(jnp.bfloat16)
    by_lane = lax.dot_general(
        order_ref[...], by_part, (((0,), (0,)), ((), ())), preferred_element_type=jnp.float32
    )
    for b in range(bands):
        piece = by_lane[:, b * LANES : (b + 1) * LANES].reshape(lanes, stacked // lanes, LANES)
        out_ref[b * lanes : (b + 1) * lanes] = piece.astype(jnp.bfloat16)


def transform_rows(scalars, pair_band, arrived, factor, lanes, rows, fields, order):
    devices, chunk_rows, _ = arrived.shape
    band_rows, points = factor.shape
    pairs = pair_band.shape[0]
    waves = 2 * pairs
    high = waves // LANES
    padded = -(-high // 8) * 8
    stacked = 2 * high * fields
    wave_band = jnp.concatenate([pair_band, pair_band[::-1]])[None, :]
    return pl.pallas_call(
        functools.partial(row_kernel, lanes, band_rows),
        in_specs=[
            pl.BlockSpec(memory_space=pltpu.VMEM),
            pl.BlockSpec(memory_space=pltpu.SMEM),
            pl.BlockSpec(memory_space=pltpu.VMEM),
            pl.BlockSpec(memory_space=pltpu.VMEM),
            pl.BlockSpec(memory_space=pltpu.VMEM),
            pl.BlockSpec(memory_space=pltpu.VMEM),
        ],
        out_specs=[pl.BlockSpec(memory_space=pltpu.VMEM)] * 2,
        scratch_shapes=[
            pltpu.VMEM((devices // lanes * LANES, waves), jnp.bfloat16),
            pltpu.VMEM((2 * rows * fields, waves), jnp.float32),
            pltpu.VMEM((2 * rows * fields, waves), jnp.float32),
            pltpu.VMEM((stacked, 2 * LANES), jnp.bfloat16),
            pltpu.VMEM((stacked, 2 * LANES), jnp.float32),
            pltpu.VMEM((1, points), jnp.float32),
            pltpu.VMEM((LANES, CHUNK), jnp.float32),
            pltpu.VMEM((LANES, CHUNK), jnp.float32),
            pltpu.VMEM((LANES, LANES), jnp.float32),
            pltpu.VMEM((LANES, LANES), jnp.float32),
            pltpu.VMEM((padded, CHUNK), jnp.float32),
            pltpu.VMEM((padded, CHUNK), jnp.float32),
            pltpu.VMEM((padded, CHUNK), jnp.float32),
            pltpu.VMEM((padded, CHUNK), jnp.float32),
        ],
        out_shape=[
            jax.ShapeDtypeStruct((rows, fields, points), jnp.bfloat16),
            jax.ShapeDtypeStruct((devices, chunk_rows, LANES), jnp.bfloat16),
        ],
    )(order, scalars, wave_band, pair_band[:, None], arrived, factor)


def on_device(coefficients, cycle_length, row_latitude, pair_band, gridpoint_factor):
    bands, lanes = lax.axis_size("band"), lax.axis_size("lon")
    devices = bands * lanes
    lane = lax.axis_index("lon")
    device = lax.axis_index("band") * lanes + lane
    own_fields, slot_count, parts, latitudes = coefficients.shape
    band_rows, points = gridpoint_factor.shape
    fields = own_fields * lanes
    own_rows = -(-band_rows // lanes)
    lane_rows = np.arange(lanes * own_rows)
    inside = np.tile(lane_rows < band_rows, bands)
    clamped = np.minimum(lane_rows, band_rows - 1)
    row_ids = (np.arange(bands)[:, None] * band_rows + clamped[None, :]).reshape(-1)
    held = row_latitude if inside.all() else jnp.take(row_latitude, row_ids)
    onehot = held[:, None] == jnp.arange(latitudes, dtype=jnp.int32)[None, :]
    own = lax.dynamic_slice_in_dim(held, device * own_rows, own_rows)
    own_places = jnp.minimum(lane * own_rows + jnp.arange(own_rows), band_rows - 1)
    scalars = jnp.concatenate([jnp.take(cycle_length, own), own_places]).astype(jnp.int32)

    leaving = jnp.einsum(
        "rl,fstl->rtfs",
        onehot.astype(jnp.bfloat16),
        coefficients,
        preferred_element_type=jnp.float32,
    ).astype(jnp.bfloat16)
    leaving = jnp.pad(leaving, ((0, 0), (0, 0), (0, 0), (0, LANES - slot_count)))
    chunk_rows = own_rows * parts * own_fields
    leaving = leaving.reshape(devices, chunk_rows, LANES)
    arrived, factor = exchange(
        gather_kernel,
        bands,
        lanes,
        0,
        [
            jax.ShapeDtypeStruct((devices, chunk_rows, LANES), jnp.bfloat16),
            jax.ShapeDtypeStruct((band_rows, lanes * points), jnp.bfloat16),
        ],
        leaving,
        gridpoint_factor,
    )

    places = np.arange(lanes * chunk_rows).reshape(lanes, own_rows, parts, own_fields)
    places = places.transpose(2, 1, 0, 3).reshape(-1)
    order = jnp.asarray(
        places[:, None] == np.arange(lanes * chunk_rows)[None, :], dtype=jnp.bfloat16
    )
    grid, result = transform_rows(
        scalars, pair_band, arrived, factor, lanes, own_rows, fields, order
    )

    blocks, returned = exchange(
        scatter_kernel,
        bands,
        lanes,
        1,
        [
            jax.ShapeDtypeStruct((lanes, own_rows, fields, points), jnp.bfloat16),
            jax.ShapeDtypeStruct((devices, chunk_rows, LANES), jnp.bfloat16),
        ],
        grid,
        result,
    )
    grid_rows = blocks.reshape(lanes * own_rows, fields, points)[:band_rows]
    grid_rows = jnp.transpose(grid_rows, (1, 0, 2))
    returned = returned.reshape(devices * own_rows, parts, own_fields, LANES)
    back = onehot & inside[:, None]
    tendencies = jnp.einsum(
        "rtfs,rl->fstl",
        returned[..., :slot_count],
        back.astype(jnp.bfloat16),
        preferred_element_type=jnp.float32,
    ).astype(jnp.bfloat16)
    return (grid_rows, tendencies)


def solution(mesh):
    return jax.shard_map(
        on_device,
        mesh=mesh,
        in_specs=(P("lon", "band", None, None), P(), P(), P(), P("band", "lon")),
        out_specs=(P(None, "band", "lon"), P("lon", "band", None, None)),
        check_vma=False,
    )
```

```python
import functools
import math

import jax
import jax.numpy as jnp
import numpy as np
from jax import lax
from jax.experimental import pallas as pl
from jax.experimental.pallas import tpu as pltpu
from jax.sharding import PartitionSpec as P

TWO_PI = 2.0 * math.pi
LANES = 128
CHUNK = 256


def cos_sin(product, length, inverse):
    turns = jnp.floor(product * inverse + 0.5)
    half = (product - turns * length) * (inverse * (0.5 * TWO_PI))
    square = half * half
    sine = jnp.full_like(half, -1.0 / math.factorial(11))
    for order in (9, 7, 5, 3, 1):
        sine = sine * square + (-1.0) ** (order // 2) / math.factorial(order)
    sine = sine * half
    cosine = jnp.full_like(half, 1.0 / math.factorial(12))
    for order in (10, 8, 6, 4, 2, 0):
        cosine = cosine * square + (-1.0) ** (order // 2) / math.factorial(order)
    return 1.0 - 2.0 * sine * sine, 2.0 * sine * cosine


MESH = pl.DeviceIdType.MESH


def round_kernel(
    bands,
    lanes,
    slot_count,
    cycle_ref,
    latitude_ref,
    order_ref,
    pair_band_ref,
    leaving,
    factor_ref,
    blocks,
    returned,
    arrived,
    cycles,
    grid_ref,
    result,
    hot,
    ordered,
    finished,
    lhs,
    total,
    row_factor,
    cos_state,
    sin_state,
    cos_step,
    sin_step,
    cos_high,
    sin_high,
    cos_high_step,
    sin_high_step,
    send_sem,
    recv_sem,
    back_send_sem,
    back_recv_sem,
    factor_send_sem,
    factor_recv_sem,
    grid_send_sem,
    grid_recv_sem,
):
    band, lane = lax.axis_index("band"), lax.axis_index("lon")
    me = band * lanes + lane
    devices = bands * lanes
    band_rows, points = factor_ref.shape
    rows, fields = grid_ref.shape[0], grid_ref.shape[1]
    slots, waves = hot.shape
    high = waves // LANES
    half = waves // 2
    stacked = leaving.shape[1] * lanes

    def peer(k):
        flat = lax.rem(me + k, devices)
        return flat, {"band": flat // lanes, "lon": lax.rem(flat, lanes)}

    def block_of(index):
        return pl.ds(pl.multiple_of(index * points, LANES), points)

    def send_chunks(source, target, sent, received):
        def send(k, carry):
            flat, device = peer(k)
            pltpu.make_async_remote_copy(
                src_ref=source.at[flat],
                dst_ref=target.at[me],
                send_sem=sent,
                recv_sem=received,
                device_id=device,
                device_id_type=MESH,
            ).start()
            return carry

        lax.fori_loop(1, devices, send, 0)
        target[me] = source[me]

    def wait_chunks(source, target, sent, received):
        pltpu.make_async_remote_copy(
            src_ref=source.at[pl.ds(0, devices - 1)],
            dst_ref=target.at[pl.ds(0, devices - 1)],
            send_sem=sent,
            recv_sem=received,
            device_id={"band": band, "lon": lane},
            device_id_type=MESH,
        ).wait()

    def factor_copy(j):
        return pltpu.make_async_remote_copy(
            src_ref=factor_ref,
            dst_ref=cycles.at[:, block_of(lane)],
            send_sem=factor_send_sem.at[j],
            recv_sem=factor_recv_sem.at[j],
            device_id={"lon": lax.rem(lane + j, lanes)},
            device_id_type=MESH,
        )

    def grid_copy(i, j):
        other = lax.rem(lane + j, lanes)
        return pltpu.make_async_remote_copy(
            src_ref=grid_ref.at[i, :, block_of(other)],
            dst_ref=blocks.at[lane, i],
            send_sem=grid_send_sem.at[i, j],
            recv_sem=grid_recv_sem.at[i, j],
            device_id={"lon": other},
            device_id_type=MESH,
        )

    barrier = pltpu.get_barrier_semaphore()

    def signal(k, carry):
        pl.semaphore_signal(barrier, inc=1, device_id=peer(k)[1], device_id_type=MESH)
        return carry

    lax.fori_loop(1, devices, signal, 0)

    pair_band = pair_band_ref[...]
    source = lax.broadcasted_iota(jnp.int32, (half, half), 0)
    target = lax.broadcasted_iota(jnp.int32, (half, half), 1)
    earlier = jnp.where(source < target, 1.0, 0.0).astype(jnp.bfloat16)
    mirror = jnp.where(source == half - 1 - target, 1.0, 0.0).astype(jnp.bfloat16)
    padded_bands = -(-bands // 8) * 8
    owner = lax.broadcasted_iota(jnp.int32, (padded_bands, half), 0) == pair_band
    counts = jnp.dot(
        jnp.where(owner, 1.0, 0.0).astype(jnp.bfloat16), earlier, preferred_element_type=jnp.float32
    )
    place = jnp.sum(jnp.where(owner, counts, 0.0), axis=0, keepdims=True)
    pair = jnp.concatenate([pair_band.astype(jnp.float32)] * 4 + [place] * 4, axis=0)
    flipped = jnp.dot(pair.astype(jnp.bfloat16), mirror, preferred_element_type=jnp.float32)
    both = jnp.concatenate([pair, flipped], axis=1)
    slot_of_wave = (both[0:1] * LANES + both[4:5]).astype(jnp.int32)

    def fill(step, carry):
        start = pl.multiple_of(step * 32, 32)
        slot = lax.broadcasted_iota(jnp.int32, (32, waves), 0) + start
        hot[pl.ds(start, 32), :] = jnp.where(slot == slot_of_wave, 1.0, 0.0).astype(jnp.bfloat16)
        return carry

    lax.fori_loop(0, slots // 32, fill, 0)

    pl.semaphore_wait(barrier, devices - 1)
    send_chunks(leaving, arrived, send_sem, recv_sem)
    for j in range(1, lanes):
        factor_copy(j).start()
    cycles[:, block_of(lane)] = factor_ref[...]

    wave = lax.broadcasted_iota(jnp.int32, (1, waves), 1)

    def length_of(i):
        row = jnp.minimum(lane * rows + i, band_rows - 1)
        n = cycle_ref[latitude_ref[band * band_rows + row]]
        length = jnp.full((1, 1), n, jnp.int32).astype(jnp.float32)
        return row, n, length, 1.0 / length

    def prepare(i, carry):
        row, n, length, inverse = length_of(i)
        low_wave = lax.broadcasted_iota(jnp.int32, (LANES, CHUNK), 0).astype(jnp.float32)
        place = lax.broadcasted_iota(jnp.int32, (LANES, CHUNK), 1).astype(jnp.float32)
        cos_state[i], sin_state[i] = cos_sin(low_wave * place, length, inverse)
        step_wave = lax.broadcasted_iota(jnp.int32, (LANES, LANES), 0).astype(jnp.float32)
        cos_step[i], sin_step[i] = cos_sin(step_wave * float(CHUNK), length, inverse)
        padded = cos_high.shape[1]
        high_wave = LANES * lax.broadcasted_iota(jnp.int32, (padded, CHUNK), 0)
        high_place = lax.broadcasted_iota(jnp.int32, (padded, CHUNK), 1)
        cos_high[i], sin_high[i] = cos_sin(
            (high_wave * high_place).astype(jnp.float32), length, inverse
        )
        cos_high_step[i], sin_high_step[i] = cos_sin(
            (high_wave * CHUNK).astype(jnp.float32), length, inverse
        )
        return carry

    lax.fori_loop(0, rows, prepare, 0)

    for j in range(1, lanes):
        factor_copy(j).wait()
    wait_chunks(leaving, arrived, send_sem, recv_sem)

    pieces = []
    for b in range(bands):
        piece = arrived[b * lanes : (b + 1) * lanes].astype(jnp.float32)
        pieces.append(piece.reshape(stacked, LANES).astype(jnp.bfloat16))
    by_part = jnp.dot(
        order_ref[...], jnp.concatenate(pieces, axis=1), preferred_element_type=jnp.float32
    ).astype(jnp.bfloat16)
    for member in range(2):
        columns = slice(member * half, (member + 1) * half)
        ordered[:, columns] = jnp.dot(
            by_part[member * stacked // 2 : (member + 1) * stacked // 2],
            hot[:, columns],
            preferred_element_type=jnp.float32,
        )

    def one_row(i, carry):
        row, n, length, inverse = length_of(i)
        norm = lax.rsqrt(length)
        kept = jnp.where(2 * wave < n, 1.0, 0.0)
        weight = kept * jnp.where(wave == 0, 1.0, 2.0)
        chosen = lax.broadcasted_iota(jnp.int32, (band_rows, 1), 0) == row
        row_factor[...] = jnp.sum(
            jnp.where(chosen, cycles[...].astype(jnp.float32), 0.0), axis=0, keepdims=True
        )
        for t in range(2):
            own = pl.ds(pl.multiple_of((t * rows + i) * fields, fields), fields)
            weighted = (ordered[own, :] * weight).astype(jnp.bfloat16)
            for b in range(high):
                part = weighted[:, b * LANES : (b + 1) * LANES]
                if t == 0:
                    lhs[b * fields : (b + 1) * fields, 0:LANES] = part
                    lhs[(high + b) * fields : (high + b + 1) * fields, LANES : 2 * LANES] = -part
                else:
                    lhs[b * fields : (b + 1) * fields, LANES : 2 * LANES] = part
                    lhs[(high + b) * fields : (high + b + 1) * fields, 0:LANES] = part

        total[...] = jnp.zeros_like(total)

        def chunk(h, carry):
            columns = pl.ds(pl.multiple_of(h * CHUNK, CHUNK), CHUNK)
            cosine, sine = cos_state[i], sin_state[i]
            table = jnp.concatenate([cosine, -sine], axis=0).astype(jnp.bfloat16)
            found = jnp.dot(lhs[...], table, preferred_element_type=jnp.float32)
            high_cos, high_sin = cos_high[i], sin_high[i]
            value = jnp.zeros((fields, CHUNK), jnp.float32)
            for b in range(high):
                real = found[b * fields : (b + 1) * fields]
                imag = found[(high + b) * fields : (high + b + 1) * fields]
                value = value + (real * high_cos[b : b + 1] - imag * high_sin[b : b + 1])
            at = h * CHUNK + lax.broadcasted_iota(jnp.int32, (1, CHUNK), 1)
            value = jnp.where(at < n, value * norm, 0.0).astype(jnp.bfloat16)
            grid_ref[i, :, columns] = value
            product = row_factor[:, columns] * value.astype(jnp.float32)
            product = product.astype(jnp.bfloat16).astype(jnp.float32)
            turned = [product * high_cos[b : b + 1] for b in range(high)]
            turned += [product * (-high_sin[b : b + 1]) for b in range(high)]
            turned = jnp.concatenate(turned, axis=0).astype(jnp.bfloat16)
            total[...] += lax.dot_general(
                turned, table, (((1,), (1,)), ((), ())), preferred_element_type=jnp.float32
            )
            step_cos = jnp.concatenate([cos_step[i]] * (CHUNK // LANES), axis=1)
            step_sin = jnp.concatenate([sin_step[i]] * (CHUNK // LANES), axis=1)
            cos_state[i] = cosine * step_cos - sine * step_sin
            sin_state[i] = sine * step_cos + cosine * step_sin
            high_step_cos, high_step_sin = cos_high_step[i], sin_high_step[i]
            cos_high[i] = high_cos * high_step_cos - high_sin * high_step_sin
            sin_high[i] = high_sin * high_step_cos + high_cos * high_step_sin
            return carry

        lax.fori_loop(0, lanes * points // CHUNK, chunk, 0)

        for j in range(1, lanes):
            grid_copy(i, j).start()
        blocks[lane, i] = grid_ref[i, :, block_of(lane)]

        scale = kept * norm
        for t in range(2):
            pieces = []
            for b in range(high):
                real = slice(b * fields, (b + 1) * fields)
                imag = slice((high + b) * fields, (high + b + 1) * fields)
                if t == 0:
                    pieces.append(total[real, 0:LANES] - total[imag, LANES : 2 * LANES])
                else:
                    pieces.append(total[imag, 0:LANES] + total[real, LANES : 2 * LANES])
            own = pl.ds(pl.multiple_of((t * rows + i) * fields, fields), fields)
            finished[own, :] = jnp.concatenate(pieces, axis=1) * scale
        return carry

    lax.fori_loop(0, rows, one_row, 0)
    pieces = []
    for member in range(2):
        columns = slice(member * half, (member + 1) * half)
        pieces.append(
            lax.dot_general(
                finished[:, columns].astype(jnp.bfloat16),
                hot[:, columns],
                (((1,), (1,)), ((), ())),
                preferred_element_type=jnp.float32,
            )
        )
    by_part = jnp.concatenate(pieces, axis=0).astype(jnp.bfloat16)
    by_lane = lax.dot_general(
        order_ref[...], by_part, (((0,), (0,)), ((), ())), preferred_element_type=jnp.float32
    )
    for b in range(bands):
        piece = by_lane[:, b * LANES : (b + 1) * LANES].reshape(lanes, stacked // lanes, LANES)
        result[b * lanes : (b + 1) * lanes] = piece.astype(jnp.bfloat16)

    send_chunks(result, returned, back_send_sem, back_recv_sem)
    for i in range(rows):
        for j in range(1, lanes):
            grid_copy(i, j).wait()
    wait_chunks(result, returned, back_send_sem, back_recv_sem)


def round_trip(cycle_length, held, order, pair_band, leaving, factor, bands, lanes, fields, slot_count):
    devices, chunk_rows, _ = leaving.shape
    band_rows, points = factor.shape
    waves = 2 * pair_band.shape[0]
    rows = -(-band_rows // lanes)
    high = waves // LANES
    padded = -(-high // 8) * 8
    stacked = 2 * high * fields
    chunks = (devices, chunk_rows, LANES)
    return pl.pallas_call(
        functools.partial(round_kernel, bands, lanes, slot_count),
        in_specs=[pl.BlockSpec(memory_space=pltpu.SMEM)] * 2
        + [pl.BlockSpec(memory_space=pltpu.VMEM)] * 4,
        out_specs=[pl.BlockSpec(memory_space=pltpu.VMEM)] * 2,
        scratch_shapes=[
            pltpu.VMEM(chunks, jnp.bfloat16),
            pltpu.VMEM((band_rows, lanes * points), jnp.bfloat16),
            pltpu.VMEM((rows, fields, lanes * points), jnp.bfloat16),
            pltpu.VMEM(chunks, jnp.bfloat16),
            pltpu.VMEM((bands * LANES, waves), jnp.bfloat16),
            pltpu.VMEM((2 * rows * fields, waves), jnp.float32),
            pltpu.VMEM((2 * rows * fields, waves), jnp.float32),
            pltpu.VMEM((stacked, 2 * LANES), jnp.bfloat16),
            pltpu.VMEM((stacked, 2 * LANES), jnp.float32),
            pltpu.VMEM((1, lanes * points), jnp.float32),
            pltpu.VMEM((rows, LANES, CHUNK), jnp.float32),
            pltpu.VMEM((rows, LANES, CHUNK), jnp.float32),
            pltpu.VMEM((rows, LANES, LANES), jnp.float32),
            pltpu.VMEM((rows, LANES, LANES), jnp.float32),
            pltpu.VMEM((rows, padded, CHUNK), jnp.float32),
            pltpu.VMEM((rows, padded, CHUNK), jnp.float32),
            pltpu.VMEM((rows, padded, CHUNK), jnp.float32),
            pltpu.VMEM((rows, padded, CHUNK), jnp.float32),
        ]
        + [pltpu.SemaphoreType.DMA] * 4
        + [pltpu.SemaphoreType.DMA((lanes,))] * 2
        + [pltpu.SemaphoreType.DMA((rows, lanes))] * 2,
        out_shape=[
            jax.ShapeDtypeStruct((lanes, rows, fields, points), jnp.bfloat16),
            jax.ShapeDtypeStruct(chunks, jnp.bfloat16),
        ],
        compiler_params=pltpu.CompilerParams(collective_id=0, has_side_effects=True),
    )(cycle_length, held, order, pair_band[None, :], leaving, factor)


def on_device(coefficients, cycle_length, row_latitude, pair_band, gridpoint_factor):
    bands, lanes = lax.axis_size("band"), lax.axis_size("lon")
    devices = bands * lanes
    own_fields, slot_count, parts, latitudes = coefficients.shape
    band_rows, points = gridpoint_factor.shape
    fields = own_fields * lanes
    own_rows = -(-band_rows // lanes)
    lane_rows = np.arange(lanes * own_rows)
    inside = np.tile(lane_rows < band_rows, bands)
    clamped = np.minimum(lane_rows, band_rows - 1)
    row_ids = (np.arange(bands)[:, None] * band_rows + clamped[None, :]).reshape(-1)
    held = row_latitude if inside.all() else jnp.take(row_latitude, row_ids)
    onehot = held[:, None] == jnp.arange(latitudes, dtype=jnp.int32)[None, :]
    leaving = jnp.einsum(
        "rl,fstl->rtfs",
        onehot.astype(jnp.bfloat16),
        coefficients,
        preferred_element_type=jnp.float32,
    ).astype(jnp.bfloat16)
    leaving = jnp.pad(leaving, ((0, 0), (0, 0), (0, 0), (0, LANES - slot_count)))
    chunk_rows = own_rows * parts * own_fields
    leaving = leaving.reshape(devices, chunk_rows, LANES)
    places = np.arange(lanes * chunk_rows).reshape(lanes, own_rows, parts, own_fields)
    places = places.transpose(2, 1, 0, 3).reshape(-1)
    order = jnp.asarray(
        places[:, None] == np.arange(lanes * chunk_rows)[None, :], dtype=jnp.bfloat16
    )
    blocks, returned = round_trip(
        cycle_length,
        row_latitude,
        order,
        pair_band,
        leaving,
        gridpoint_factor,
        bands,
        lanes,
        fields,
        slot_count,
    )
    grid_rows = blocks.reshape(lanes * own_rows, fields, points)[:band_rows]
    grid_rows = jnp.transpose(grid_rows, (1, 0, 2))
    returned = returned.reshape(devices * own_rows, parts, own_fields, LANES)
    back = onehot & inside[:, None]
    tendencies = jnp.einsum(
        "rtfs,rl->fstl",
        returned[..., :slot_count],
        back.astype(jnp.bfloat16),
        preferred_element_type=jnp.float32,
    ).astype(jnp.bfloat16)
    return (grid_rows, tendencies)


def solution(mesh):
    return jax.shard_map(
        on_device,
        mesh=mesh,
        in_specs=(P("lon", "band", None, None), P(), P(), P(), P("band", "lon")),
        out_specs=(P(None, "band", "lon"), P("lon", "band", None, None)),
        check_vma=False,
    )
```

```python
import functools
import math

import jax
import jax.numpy as jnp
import numpy as np
from jax import lax
from jax.experimental import pallas as pl
from jax.experimental.pallas import tpu as pltpu
from jax.sharding import PartitionSpec as P

TWO_PI = 2.0 * math.pi
LANES = 128
CHUNK = 256


def cos_sin(product, length, inverse):
    turns = jnp.floor(product * inverse + 0.5)
    half = (product - turns * length) * (inverse * (0.5 * TWO_PI))
    square = half * half
    sine = jnp.full_like(half, -1.0 / math.factorial(11))
    for order in (9, 7, 5, 3, 1):
        sine = sine * square + (-1.0) ** (order // 2) / math.factorial(order)
    sine = sine * half
    cosine = jnp.full_like(half, 1.0 / math.factorial(12))
    for order in (10, 8, 6, 4, 2, 0):
        cosine = cosine * square + (-1.0) ** (order // 2) / math.factorial(order)
    return 1.0 - 2.0 * sine * sine, 2.0 * sine * cosine


MESH = pl.DeviceIdType.MESH


def round_kernel(
    bands,
    lanes,
    cycle_ref,
    latitude_ref,
    order_ref,
    pair_band_ref,
    leaving,
    factor_ref,
    blocks,
    returned,
    arrived,
    cycles,
    grid_ref,
    result,
    hot,
    ordered,
    finished,
    lhs,
    total,
    row_factor,
    cos_state,
    sin_state,
    cos_step,
    sin_step,
    cos_high,
    sin_high,
    cos_high_step,
    sin_high_step,
    send_sem,
    recv_sem,
    back_send_sem,
    back_recv_sem,
    factor_send_sem,
    factor_recv_sem,
    grid_send_sem,
    grid_recv_sem,
):
    band, lane = lax.axis_index("band"), lax.axis_index("lon")
    me = band * lanes + lane
    devices = bands * lanes
    band_rows, points = factor_ref.shape
    rows, fields = grid_ref.shape[0], grid_ref.shape[1]
    slots, waves = hot.shape
    high = waves // LANES
    half = waves // 2
    stacked = leaving.shape[1] * lanes

    def peer(k):
        flat = lax.rem(me + k, devices)
        return flat, {"band": flat // lanes, "lon": lax.rem(flat, lanes)}

    def block_of(index):
        return pl.ds(pl.multiple_of(index * points, LANES), points)

    def send_chunks(source, target, sent, received):
        def send(k, carry):
            flat, device = peer(k)
            pltpu.make_async_remote_copy(
                src_ref=source.at[flat],
                dst_ref=target.at[me],
                send_sem=sent,
                recv_sem=received,
                device_id=device,
                device_id_type=MESH,
            ).start()
            return carry

        lax.fori_loop(1, devices, send, 0)
        target[me] = source[me]

    def wait_chunks(source, target, sent, received):
        pltpu.make_async_remote_copy(
            src_ref=source.at[pl.ds(0, devices - 1)],
            dst_ref=target.at[pl.ds(0, devices - 1)],
            send_sem=sent,
            recv_sem=received,
            device_id={"band": band, "lon": lane},
            device_id_type=MESH,
        ).wait()

    def factor_copy(j):
        return pltpu.make_async_remote_copy(
            src_ref=factor_ref,
            dst_ref=cycles.at[:, block_of(lane)],
            send_sem=factor_send_sem.at[j],
            recv_sem=factor_recv_sem.at[j],
            device_id={"lon": lax.rem(lane + j, lanes)},
            device_id_type=MESH,
        )

    def grid_copy(i, j):
        other = lax.rem(lane + j, lanes)
        return pltpu.make_async_remote_copy(
            src_ref=grid_ref.at[i, :, block_of(other)],
            dst_ref=blocks.at[lane, i],
            send_sem=grid_send_sem.at[i, j],
            recv_sem=grid_recv_sem.at[i, j],
            device_id={"lon": other},
            device_id_type=MESH,
        )

    barrier = pltpu.get_barrier_semaphore()

    def signal(k, carry):
        pl.semaphore_signal(barrier, inc=1, device_id=peer(k)[1], device_id_type=MESH)
        return carry

    lax.fori_loop(1, devices, signal, 0)

    pair_band = pair_band_ref[...].reshape(1, half)
    source = lax.broadcasted_iota(jnp.int32, (half, half), 0)
    target = lax.broadcasted_iota(jnp.int32, (half, half), 1)
    earlier = jnp.where(source < target, 1.0, 0.0).astype(jnp.bfloat16)
    mirror = jnp.where(source == half - 1 - target, 1.0, 0.0).astype(jnp.bfloat16)
    padded_bands = -(-bands // 8) * 8
    owner = lax.broadcasted_iota(jnp.int32, (padded_bands, half), 0) == pair_band
    counts = jnp.dot(
        jnp.where(owner, 1.0, 0.0).astype(jnp.bfloat16), earlier, preferred_element_type=jnp.float32
    )
    place = jnp.sum(jnp.where(owner, counts, 0.0), axis=0, keepdims=True)
    pair = jnp.concatenate([pair_band.astype(jnp.float32)] * 4 + [place] * 4, axis=0)
    flipped = jnp.dot(pair.astype(jnp.bfloat16), mirror, preferred_element_type=jnp.float32)
    both = jnp.concatenate([pair, flipped], axis=1)
    slot_of_wave = (both[0:1] * LANES + both[4:5]).astype(jnp.int32)

    def fill(step, carry):
        start = pl.multiple_of(step * 32, 32)
        slot = lax.broadcasted_iota(jnp.int32, (32, waves), 0) + start
        hot[pl.ds(start, 32), :] = jnp.where(slot == slot_of_wave, 1.0, 0.0).astype(jnp.bfloat16)
        return carry

    lax.fori_loop(0, slots // 32, fill, 0)

    pl.semaphore_wait(barrier, devices - 1)
    send_chunks(leaving, arrived, send_sem, recv_sem)
    for j in range(1, lanes):
        factor_copy(j).start()
    cycles[:, block_of(lane)] = factor_ref[...]

    wave = lax.broadcasted_iota(jnp.int32, (1, waves), 1)

    def length_of(i):
        row = jnp.minimum(lane * rows + i, band_rows - 1)
        n = cycle_ref[latitude_ref[band * band_rows + row]]
        length = jnp.full((1, 1), n, jnp.int32).astype(jnp.float32)
        return row, n, length, 1.0 / length

    def prepare(i, carry):
        row, n, length, inverse = length_of(i)
        low_wave = lax.broadcasted_iota(jnp.int32, (LANES, CHUNK), 0).astype(jnp.float32)
        place = lax.broadcasted_iota(jnp.int32, (LANES, CHUNK), 1).astype(jnp.float32)
        cos_state[i], sin_state[i] = cos_sin(low_wave * place, length, inverse)
        step_wave = lax.broadcasted_iota(jnp.int32, (LANES, LANES), 0).astype(jnp.float32)
        cos_step[i], sin_step[i] = cos_sin(step_wave * float(CHUNK), length, inverse)
        padded = cos_high.shape[1]
        high_wave = LANES * lax.broadcasted_iota(jnp.int32, (padded, CHUNK), 0)
        high_place = lax.broadcasted_iota(jnp.int32, (padded, CHUNK), 1)
        cos_high[i], sin_high[i] = cos_sin(
            (high_wave * high_place).astype(jnp.float32), length, inverse
        )
        cos_high_step[i], sin_high_step[i] = cos_sin(
            (high_wave * CHUNK).astype(jnp.float32), length, inverse
        )
        return carry

    lax.fori_loop(0, rows, prepare, 0)

    wait_chunks(leaving, arrived, send_sem, recv_sem)

    pieces = []
    for b in range(bands):
        piece = arrived[b * lanes : (b + 1) * lanes].astype(jnp.float32)
        pieces.append(piece.reshape(stacked, LANES).astype(jnp.bfloat16))
    by_part = jnp.dot(
        order_ref[...], jnp.concatenate(pieces, axis=1), preferred_element_type=jnp.float32
    ).astype(jnp.bfloat16)
    for member in range(2):
        columns = slice(member * half, (member + 1) * half)
        ordered[:, columns] = jnp.dot(
            by_part[member * stacked // 2 : (member + 1) * stacked // 2],
            hot[:, columns],
            preferred_element_type=jnp.float32,
        )

    for j in range(1, lanes):
        factor_copy(j).wait()

    def one_row(i, carry):
        row, n, length, inverse = length_of(i)
        norm = lax.rsqrt(length)
        kept = jnp.where(2 * wave < n, 1.0, 0.0)
        weight = kept * jnp.where(wave == 0, 1.0, 2.0)
        chosen = lax.broadcasted_iota(jnp.int32, (band_rows, 1), 0) == row
        row_factor[...] = jnp.sum(
            jnp.where(chosen, cycles[...].astype(jnp.float32), 0.0), axis=0, keepdims=True
        )
        for t in range(2):
            own = pl.ds(pl.multiple_of((t * rows + i) * fields, fields), fields)
            weighted = (ordered[own, :] * weight).astype(jnp.bfloat16)
            for b in range(high):
                part = weighted[:, b * LANES : (b + 1) * LANES]
                if t == 0:
                    lhs[b * fields : (b + 1) * fields, 0:LANES] = part
                    lhs[(high + b) * fields : (high + b + 1) * fields, LANES : 2 * LANES] = -part
                else:
                    lhs[b * fields : (b + 1) * fields, LANES : 2 * LANES] = part
                    lhs[(high + b) * fields : (high + b + 1) * fields, 0:LANES] = part

        total[...] = jnp.zeros_like(total)

        def chunk(h, carry):
            columns = pl.ds(pl.multiple_of(h * CHUNK, CHUNK), CHUNK)
            cosine, sine = cos_state[i], sin_state[i]
            table = jnp.concatenate([cosine, -sine], axis=0).astype(jnp.bfloat16)
            found = jnp.dot(lhs[...], table, preferred_element_type=jnp.float32)
            high_cos, high_sin = cos_high[i], sin_high[i]
            value = jnp.zeros((fields, CHUNK), jnp.float32)
            for b in range(high):
                real = found[b * fields : (b + 1) * fields]
                imag = found[(high + b) * fields : (high + b + 1) * fields]
                value = value + (real * high_cos[b : b + 1] - imag * high_sin[b : b + 1])
            at = h * CHUNK + lax.broadcasted_iota(jnp.int32, (1, CHUNK), 1)
            value = jnp.where(at < n, value * norm, 0.0).astype(jnp.bfloat16)
            grid_ref[i, :, columns] = value
            product = row_factor[:, columns] * value.astype(jnp.float32)
            product = product.astype(jnp.bfloat16).astype(jnp.float32)
            turned = [product * high_cos[b : b + 1] for b in range(high)]
            turned += [product * (-high_sin[b : b + 1]) for b in range(high)]
            turned = jnp.concatenate(turned, axis=0).astype(jnp.bfloat16)
            total[...] += lax.dot_general(
                turned, table, (((1,), (1,)), ((), ())), preferred_element_type=jnp.float32
            )
            step_cos = jnp.concatenate([cos_step[i]] * (CHUNK // LANES), axis=1)
            step_sin = jnp.concatenate([sin_step[i]] * (CHUNK // LANES), axis=1)
            cos_state[i] = cosine * step_cos - sine * step_sin
            sin_state[i] = sine * step_cos + cosine * step_sin
            high_step_cos, high_step_sin = cos_high_step[i], sin_high_step[i]
            cos_high[i] = high_cos * high_step_cos - high_sin * high_step_sin
            sin_high[i] = high_sin * high_step_cos + high_cos * high_step_sin
            return carry

        lax.fori_loop(0, lanes * points // CHUNK, chunk, 0, unroll=True)

        for j in range(1, lanes):
            grid_copy(i, j).start()
        blocks[lane, i] = grid_ref[i, :, block_of(lane)]

        scale = kept * norm
        for t in range(2):
            pieces = []
            for b in range(high):
                real = slice(b * fields, (b + 1) * fields)
                imag = slice((high + b) * fields, (high + b + 1) * fields)
                if t == 0:
                    pieces.append(total[real, 0:LANES] - total[imag, LANES : 2 * LANES])
                else:
                    pieces.append(total[imag, 0:LANES] + total[real, LANES : 2 * LANES])
            own = pl.ds(pl.multiple_of((t * rows + i) * fields, fields), fields)
            finished[own, :] = jnp.concatenate(pieces, axis=1) * scale
        return carry

    lax.fori_loop(0, rows, one_row, 0)
    pieces = []
    for member in range(2):
        columns = slice(member * half, (member + 1) * half)
        pieces.append(
            lax.dot_general(
                finished[:, columns].astype(jnp.bfloat16),
                hot[:, columns],
                (((1,), (1,)), ((), ())),
                preferred_element_type=jnp.float32,
            )
        )
    by_part = jnp.concatenate(pieces, axis=0).astype(jnp.bfloat16)
    by_lane = lax.dot_general(
        order_ref[...], by_part, (((0,), (0,)), ((), ())), preferred_element_type=jnp.float32
    )
    for b in range(bands):
        piece = by_lane[:, b * LANES : (b + 1) * LANES].reshape(lanes, stacked // lanes, LANES)
        result[b * lanes : (b + 1) * lanes] = piece.astype(jnp.bfloat16)

    send_chunks(result, returned, back_send_sem, back_recv_sem)
    for i in range(rows):
        for j in range(1, lanes):
            grid_copy(i, j).wait()
    wait_chunks(result, returned, back_send_sem, back_recv_sem)


def round_trip(cycle_length, held, order, pair_band, leaving, factor, bands, lanes, fields):
    devices, chunk_rows, _ = leaving.shape
    band_rows, points = factor.shape
    waves = 2 * pair_band.shape[0]
    rows = -(-band_rows // lanes)
    high = waves // LANES
    padded = -(-high // 8) * 8
    stacked = 2 * high * fields
    chunks = (devices, chunk_rows, LANES)
    return pl.pallas_call(
        functools.partial(round_kernel, bands, lanes),
        in_specs=[pl.BlockSpec(memory_space=pltpu.SMEM)] * 2
        + [pl.BlockSpec(memory_space=pltpu.VMEM)] * 4,
        out_specs=[pl.BlockSpec(memory_space=pltpu.VMEM)] * 2,
        scratch_shapes=[
            pltpu.VMEM(chunks, jnp.bfloat16),
            pltpu.VMEM((band_rows, lanes * points), jnp.bfloat16),
            pltpu.VMEM((rows, fields, lanes * points), jnp.bfloat16),
            pltpu.VMEM(chunks, jnp.bfloat16),
            pltpu.VMEM((bands * LANES, waves), jnp.bfloat16),
            pltpu.VMEM((2 * rows * fields, waves), jnp.float32),
            pltpu.VMEM((2 * rows * fields, waves), jnp.float32),
            pltpu.VMEM((stacked, 2 * LANES), jnp.bfloat16),
            pltpu.VMEM((stacked, 2 * LANES), jnp.float32),
            pltpu.VMEM((1, lanes * points), jnp.float32),
            pltpu.VMEM((rows, LANES, CHUNK), jnp.float32),
            pltpu.VMEM((rows, LANES, CHUNK), jnp.float32),
            pltpu.VMEM((rows, LANES, LANES), jnp.float32),
            pltpu.VMEM((rows, LANES, LANES), jnp.float32),
            pltpu.VMEM((rows, padded, CHUNK), jnp.float32),
            pltpu.VMEM((rows, padded, CHUNK), jnp.float32),
            pltpu.VMEM((rows, padded, CHUNK), jnp.float32),
            pltpu.VMEM((rows, padded, CHUNK), jnp.float32),
        ]
        + [pltpu.SemaphoreType.DMA] * 4
        + [pltpu.SemaphoreType.DMA((lanes,))] * 2
        + [pltpu.SemaphoreType.DMA((rows, lanes))] * 2,
        out_shape=[
            jax.ShapeDtypeStruct((lanes, rows, fields, points), jnp.bfloat16),
            jax.ShapeDtypeStruct(chunks, jnp.bfloat16),
        ],
        compiler_params=pltpu.CompilerParams(
            collective_id=0,
            has_side_effects=True,
            vmem_limit_bytes=(12 << 20) + 4 * bands * LANES * waves,
        ),
    )(cycle_length, held, order, pair_band, leaving, factor)


def on_device(coefficients, cycle_length, row_latitude, pair_band, gridpoint_factor):
    bands, lanes = lax.axis_size("band"), lax.axis_size("lon")
    devices = bands * lanes
    own_fields, slot_count, parts, latitudes = coefficients.shape
    band_rows, points = gridpoint_factor.shape
    fields = own_fields * lanes
    own_rows = -(-band_rows // lanes)
    lane_rows = np.arange(lanes * own_rows)
    inside = np.tile(lane_rows < band_rows, bands)
    clamped = np.minimum(lane_rows, band_rows - 1)
    row_ids = (np.arange(bands)[:, None] * band_rows + clamped[None, :]).reshape(-1)
    held = row_latitude if inside.all() else jnp.take(row_latitude, row_ids)
    onehot = held[:, None] == jnp.arange(latitudes, dtype=jnp.int32)[None, :]
    leaving = jnp.einsum(
        "rl,fstl->rtfs",
        onehot.astype(jnp.bfloat16),
        coefficients,
        preferred_element_type=jnp.float32,
    ).astype(jnp.bfloat16)
    leaving = jnp.pad(leaving, ((0, 0), (0, 0), (0, 0), (0, LANES - slot_count)))
    chunk_rows = own_rows * parts * own_fields
    leaving = leaving.reshape(devices, chunk_rows, LANES)
    places = np.arange(lanes * chunk_rows).reshape(lanes, own_rows, parts, own_fields)
    places = places.transpose(2, 1, 0, 3).reshape(-1)
    order = jnp.asarray(
        places[:, None] == np.arange(lanes * chunk_rows)[None, :], dtype=jnp.bfloat16
    )
    blocks, returned = round_trip(
        cycle_length,
        row_latitude,
        order,
        pair_band,
        leaving,
        gridpoint_factor,
        bands,
        lanes,
        fields,
    )
    grid_rows = blocks.reshape(lanes * own_rows, fields, points)[:band_rows]
    grid_rows = jnp.transpose(grid_rows, (1, 0, 2))
    returned = returned.reshape(devices * own_rows, parts, own_fields, LANES)
    back = onehot & inside[:, None]
    tendencies = jnp.einsum(
        "rtfs,rl->fstl",
        returned[..., :slot_count],
        back.astype(jnp.bfloat16),
        preferred_element_type=jnp.float32,
    ).astype(jnp.bfloat16)
    return (grid_rows, tendencies)


def solution(mesh):
    return jax.shard_map(
        on_device,
        mesh=mesh,
        in_specs=(P("lon", "band", None, None), P(), P(), P(), P("band", "lon")),
        out_specs=(P(None, "band", "lon"), P("lon", "band", None, None)),
        check_vma=False,
    )
```

```python
import functools
import math

import jax
import jax.numpy as jnp
import numpy as np
from jax import lax
from jax.experimental import pallas as pl
from jax.experimental.pallas import tpu as pltpu
from jax.sharding import PartitionSpec as P

TWO_PI = 2.0 * math.pi
LANES = 128
CHUNK = 256


def cos_sin(product, length, inverse):
    turns = jnp.floor(product * inverse + 0.5)
    half = (product - turns * length) * (inverse * (0.5 * TWO_PI))
    square = half * half
    sine = jnp.full_like(half, -1.0 / math.factorial(11))
    for order in (9, 7, 5, 3, 1):
        sine = sine * square + (-1.0) ** (order // 2) / math.factorial(order)
    sine = sine * half
    cosine = jnp.full_like(half, 1.0 / math.factorial(12))
    for order in (10, 8, 6, 4, 2, 0):
        cosine = cosine * square + (-1.0) ** (order // 2) / math.factorial(order)
    return 1.0 - 2.0 * sine * sine, 2.0 * sine * cosine


MESH = pl.DeviceIdType.MESH


def round_kernel(
    bands,
    lanes,
    cycle_ref,
    latitude_ref,
    order_ref,
    pair_band_ref,
    leaving,
    factor_ref,
    blocks,
    returned,
    arrived,
    cycles,
    grid_ref,
    result,
    hot,
    ordered,
    finished,
    lhs,
    total,
    row_factor,
    cos_state,
    sin_state,
    cos_step,
    sin_step,
    cos_high,
    sin_high,
    cos_high_step,
    sin_high_step,
    send_sem,
    recv_sem,
    back_send_sem,
    back_recv_sem,
    factor_send_sem,
    factor_recv_sem,
    grid_send_sem,
    grid_recv_sem,
):
    band, lane = lax.axis_index("band"), lax.axis_index("lon")
    me = band * lanes + lane
    devices = bands * lanes
    band_rows, points = factor_ref.shape
    rows, fields = grid_ref.shape[0], grid_ref.shape[1]
    slots, waves = hot.shape
    high = waves // LANES
    half = waves // 2
    stacked = leaving.shape[1] * lanes

    def peer(k):
        flat = lax.rem(me + k, devices)
        return flat, {"band": flat // lanes, "lon": lax.rem(flat, lanes)}

    def block_of(index):
        return pl.ds(pl.multiple_of(index * points, LANES), points)

    def send_chunks(source, target, sent, received):
        def send(k, carry):
            flat, device = peer(k)
            pltpu.make_async_remote_copy(
                src_ref=source.at[flat],
                dst_ref=target.at[me],
                send_sem=sent,
                recv_sem=received,
                device_id=device,
                device_id_type=MESH,
            ).start()
            return carry

        lax.fori_loop(1, devices, send, 0)
        target[me] = source[me]

    def wait_chunks(source, target, sent, received):
        pltpu.make_async_remote_copy(
            src_ref=source.at[pl.ds(0, devices - 1)],
            dst_ref=target.at[pl.ds(0, devices - 1)],
            send_sem=sent,
            recv_sem=received,
            device_id={"band": band, "lon": lane},
            device_id_type=MESH,
        ).wait()

    def factor_copy(j):
        return pltpu.make_async_remote_copy(
            src_ref=factor_ref,
            dst_ref=cycles.at[:, block_of(lane)],
            send_sem=factor_send_sem.at[j],
            recv_sem=factor_recv_sem.at[j],
            device_id={"lon": lax.rem(lane + j, lanes)},
            device_id_type=MESH,
        )

    def grid_copy(i, j):
        other = lax.rem(lane + j, lanes)
        return pltpu.make_async_remote_copy(
            src_ref=grid_ref.at[i, :, block_of(other)],
            dst_ref=blocks.at[lane, i],
            send_sem=grid_send_sem.at[i, j],
            recv_sem=grid_recv_sem.at[i, j],
            device_id={"lon": other},
            device_id_type=MESH,
        )

    barrier = pltpu.get_barrier_semaphore()

    def signal(k, carry):
        pl.semaphore_signal(barrier, inc=1, device_id=peer(k)[1], device_id_type=MESH)
        return carry

    lax.fori_loop(1, devices, signal, 0)

    pair_band = pair_band_ref[...].reshape(1, half)
    source = lax.broadcasted_iota(jnp.int32, (half, half), 0)
    target = lax.broadcasted_iota(jnp.int32, (half, half), 1)
    earlier = jnp.where(source < target, 1.0, 0.0).astype(jnp.bfloat16)
    mirror = jnp.where(source == half - 1 - target, 1.0, 0.0).astype(jnp.bfloat16)
    padded_bands = -(-bands // 8) * 8
    owner = lax.broadcasted_iota(jnp.int32, (padded_bands, half), 0) == pair_band
    counts = jnp.dot(
        jnp.where(owner, 1.0, 0.0).astype(jnp.bfloat16), earlier, preferred_element_type=jnp.float32
    )
    place = jnp.sum(jnp.where(owner, counts, 0.0), axis=0, keepdims=True)
    pair = jnp.concatenate([pair_band.astype(jnp.float32)] * 4 + [place] * 4, axis=0)
    flipped = jnp.dot(pair.astype(jnp.bfloat16), mirror, preferred_element_type=jnp.float32)
    both = jnp.concatenate([pair, flipped], axis=1)
    slot_of_wave = (both[0:1] * LANES + both[4:5]).astype(jnp.int32)

    def fill(step, carry):
        start = pl.multiple_of(step * 32, 32)
        slot = lax.broadcasted_iota(jnp.int32, (32, waves), 0) + start
        hot[pl.ds(start, 32), :] = jnp.where(slot == slot_of_wave, 1.0, 0.0).astype(jnp.bfloat16)
        return carry

    lax.fori_loop(0, slots // 32, fill, 0)

    pl.semaphore_wait(barrier, devices - 1)
    send_chunks(leaving, arrived, send_sem, recv_sem)
    for j in range(1, lanes):
        factor_copy(j).start()
    cycles[:, block_of(lane)] = factor_ref[...]

    wave = lax.broadcasted_iota(jnp.int32, (1, waves), 1)

    def length_of(i):
        row = jnp.minimum(lane * rows + i, band_rows - 1)
        n = cycle_ref[latitude_ref[band * band_rows + row]]
        length = jnp.full((1, 1), n, jnp.int32).astype(jnp.float32)
        return row, n, length, 1.0 / length

    def prepare(i, carry):
        row, n, length, inverse = length_of(i)
        low_wave = lax.broadcasted_iota(jnp.int32, (LANES, CHUNK), 0).astype(jnp.float32)
        place = lax.broadcasted_iota(jnp.int32, (LANES, CHUNK), 1).astype(jnp.float32)
        cos_state[i], sin_state[i] = cos_sin(low_wave * place, length, inverse)
        step_wave = lax.broadcasted_iota(jnp.int32, (LANES, LANES), 0).astype(jnp.float32)
        cos_step[i], sin_step[i] = cos_sin(step_wave * float(CHUNK), length, inverse)
        padded = cos_high.shape[1]
        high_wave = LANES * lax.broadcasted_iota(jnp.int32, (padded, CHUNK), 0)
        high_place = lax.broadcasted_iota(jnp.int32, (padded, CHUNK), 1)
        cos_high[i], sin_high[i] = cos_sin(
            (high_wave * high_place).astype(jnp.float32), length, inverse
        )
        cos_high_step[i], sin_high_step[i] = cos_sin(
            (high_wave * CHUNK).astype(jnp.float32), length, inverse
        )
        return carry

    lax.fori_loop(0, rows, prepare, 0)

    wait_chunks(leaving, arrived, send_sem, recv_sem)

    pieces = []
    for b in range(bands):
        piece = arrived[b * lanes : (b + 1) * lanes].astype(jnp.float32)
        pieces.append(piece.reshape(stacked, LANES).astype(jnp.bfloat16))
    by_part = jnp.dot(
        order_ref[...], jnp.concatenate(pieces, axis=1), preferred_element_type=jnp.float32
    ).astype(jnp.bfloat16)
    for member in range(2):
        columns = slice(member * half, (member + 1) * half)
        ordered[:, columns] = jnp.dot(
            by_part[member * stacked // 2 : (member + 1) * stacked // 2],
            hot[:, columns],
            preferred_element_type=jnp.float32,
        )

    for j in range(1, lanes):
        factor_copy(j).wait()

    def one_row(i, carry):
        row, n, length, inverse = length_of(i)
        norm = lax.rsqrt(length)
        kept = jnp.where(2 * wave < n, 1.0, 0.0)
        weight = kept * jnp.where(wave == 0, 1.0, 2.0)
        chosen = lax.broadcasted_iota(jnp.int32, (band_rows, 1), 0) == row
        row_factor[...] = jnp.sum(
            jnp.where(chosen, cycles[...].astype(jnp.float32), 0.0), axis=0, keepdims=True
        )
        for t in range(2):
            own = pl.ds(pl.multiple_of((t * rows + i) * fields, fields), fields)
            weighted = (ordered[own, :] * weight).astype(jnp.bfloat16)
            for b in range(high):
                part = weighted[:, b * LANES : (b + 1) * LANES]
                if t == 0:
                    lhs[b * fields : (b + 1) * fields, 0:LANES] = part
                    lhs[(high + b) * fields : (high + b + 1) * fields, LANES : 2 * LANES] = -part
                else:
                    lhs[b * fields : (b + 1) * fields, LANES : 2 * LANES] = part
                    lhs[(high + b) * fields : (high + b + 1) * fields, 0:LANES] = part

        total[...] = jnp.zeros_like(total)

        def chunk(h, carry):
            columns = pl.ds(pl.multiple_of(h * CHUNK, CHUNK), CHUNK)
            cosine, sine = cos_state[i], sin_state[i]
            table = jnp.concatenate([cosine, -sine], axis=0).astype(jnp.bfloat16)
            found = jnp.dot(lhs[...], table, preferred_element_type=jnp.float32)
            high_cos, high_sin = cos_high[i], sin_high[i]
            value = jnp.zeros((fields, CHUNK), jnp.float32)
            for b in range(high):
                real = found[b * fields : (b + 1) * fields]
                imag = found[(high + b) * fields : (high + b + 1) * fields]
                value = value + (real * high_cos[b : b + 1] - imag * high_sin[b : b + 1])
            at = h * CHUNK + lax.broadcasted_iota(jnp.int32, (1, CHUNK), 1)
            value = jnp.where(at < n, value * norm, 0.0).astype(jnp.bfloat16)
            grid_ref[i, :, columns] = value
            product = row_factor[:, columns] * value.astype(jnp.float32)
            product = product.astype(jnp.bfloat16).astype(jnp.float32)
            turned = [product * high_cos[b : b + 1] for b in range(high)]
            turned += [product * (-high_sin[b : b + 1]) for b in range(high)]
            turned = jnp.concatenate(turned, axis=0).astype(jnp.bfloat16)
            total[...] += lax.dot_general(
                turned, table, (((1,), (1,)), ((), ())), preferred_element_type=jnp.float32
            )
            step_cos = jnp.concatenate([cos_step[i]] * (CHUNK // LANES), axis=1)
            step_sin = jnp.concatenate([sin_step[i]] * (CHUNK // LANES), axis=1)
            cos_state[i] = cosine * step_cos - sine * step_sin
            sin_state[i] = sine * step_cos + cosine * step_sin
            high_step_cos, high_step_sin = cos_high_step[i], sin_high_step[i]
            cos_high[i] = high_cos * high_step_cos - high_sin * high_step_sin
            sin_high[i] = high_sin * high_step_cos + high_cos * high_step_sin
            return carry

        lax.fori_loop(0, lanes * points // CHUNK, chunk, 0, unroll=True)

        for j in range(1, lanes):
            grid_copy(i, j).start()
        blocks[lane, i] = grid_ref[i, :, block_of(lane)]

        scale = kept * norm
        for t in range(2):
            pieces = []
            for b in range(high):
                real = slice(b * fields, (b + 1) * fields)
                imag = slice((high + b) * fields, (high + b + 1) * fields)
                if t == 0:
                    pieces.append(total[real, 0:LANES] - total[imag, LANES : 2 * LANES])
                else:
                    pieces.append(total[imag, 0:LANES] + total[real, LANES : 2 * LANES])
            own = pl.ds(pl.multiple_of((t * rows + i) * fields, fields), fields)
            finished[own, :] = jnp.concatenate(pieces, axis=1) * scale
        return carry

    lax.fori_loop(0, rows, one_row, 0, unroll=True)
    pieces = []
    for member in range(2):
        columns = slice(member * half, (member + 1) * half)
        pieces.append(
            lax.dot_general(
                finished[:, columns].astype(jnp.bfloat16),
                hot[:, columns],
                (((1,), (1,)), ((), ())),
                preferred_element_type=jnp.float32,
            )
        )
    by_part = jnp.concatenate(pieces, axis=0).astype(jnp.bfloat16)
    by_lane = lax.dot_general(
        order_ref[...], by_part, (((0,), (0,)), ((), ())), preferred_element_type=jnp.float32
    )
    for b in range(bands):
        piece = by_lane[:, b * LANES : (b + 1) * LANES].reshape(lanes, stacked // lanes, LANES)
        result[b * lanes : (b + 1) * lanes] = piece.astype(jnp.bfloat16)

    send_chunks(result, returned, back_send_sem, back_recv_sem)
    for i in range(rows):
        for j in range(1, lanes):
            grid_copy(i, j).wait()
    wait_chunks(result, returned, back_send_sem, back_recv_sem)


def round_trip(cycle_length, held, order, pair_band, leaving, factor, bands, lanes, fields):
    devices, chunk_rows, _ = leaving.shape
    band_rows, points = factor.shape
    waves = 2 * pair_band.shape[0]
    rows = -(-band_rows // lanes)
    high = waves // LANES
    padded = -(-high // 8) * 8
    stacked = 2 * high * fields
    chunks = (devices, chunk_rows, LANES)
    return pl.pallas_call(
        functools.partial(round_kernel, bands, lanes),
        in_specs=[pl.BlockSpec(memory_space=pltpu.SMEM)] * 2
        + [pl.BlockSpec(memory_space=pltpu.VMEM)] * 4,
        out_specs=[pl.BlockSpec(memory_space=pltpu.VMEM)] * 2,
        scratch_shapes=[
            pltpu.VMEM(chunks, jnp.bfloat16),
            pltpu.VMEM((band_rows, lanes * points), jnp.bfloat16),
            pltpu.VMEM((rows, fields, lanes * points), jnp.bfloat16),
            pltpu.VMEM(chunks, jnp.bfloat16),
            pltpu.VMEM((bands * LANES, waves), jnp.bfloat16),
            pltpu.VMEM((2 * rows * fields, waves), jnp.float32),
            pltpu.VMEM((2 * rows * fields, waves), jnp.float32),
            pltpu.VMEM((stacked, 2 * LANES), jnp.bfloat16),
            pltpu.VMEM((stacked, 2 * LANES), jnp.float32),
            pltpu.VMEM((1, lanes * points), jnp.float32),
            pltpu.VMEM((rows, LANES, CHUNK), jnp.float32),
            pltpu.VMEM((rows, LANES, CHUNK), jnp.float32),
            pltpu.VMEM((rows, LANES, LANES), jnp.float32),
            pltpu.VMEM((rows, LANES, LANES), jnp.float32),
            pltpu.VMEM((rows, padded, CHUNK), jnp.float32),
            pltpu.VMEM((rows, padded, CHUNK), jnp.float32),
            pltpu.VMEM((rows, padded, CHUNK), jnp.float32),
            pltpu.VMEM((rows, padded, CHUNK), jnp.float32),
        ]
        + [pltpu.SemaphoreType.DMA] * 4
        + [pltpu.SemaphoreType.DMA((lanes,))] * 2
        + [pltpu.SemaphoreType.DMA((rows, lanes))] * 2,
        out_shape=[
            jax.ShapeDtypeStruct((lanes, rows, fields, points), jnp.bfloat16),
            jax.ShapeDtypeStruct(chunks, jnp.bfloat16),
        ],
        compiler_params=pltpu.CompilerParams(
            collective_id=0,
            has_side_effects=True,
            vmem_limit_bytes=(12 << 20) + 4 * bands * LANES * waves,
        ),
    )(cycle_length, held, order, pair_band, leaving, factor)


def on_device(coefficients, cycle_length, row_latitude, pair_band, gridpoint_factor):
    bands, lanes = lax.axis_size("band"), lax.axis_size("lon")
    devices = bands * lanes
    own_fields, slot_count, parts, latitudes = coefficients.shape
    band_rows, points = gridpoint_factor.shape
    fields = own_fields * lanes
    own_rows = -(-band_rows // lanes)
    lane_rows = np.arange(lanes * own_rows)
    inside = np.tile(lane_rows < band_rows, bands)
    clamped = np.minimum(lane_rows, band_rows - 1)
    row_ids = (np.arange(bands)[:, None] * band_rows + clamped[None, :]).reshape(-1)
    held = row_latitude if inside.all() else jnp.take(row_latitude, row_ids)
    onehot = held[:, None] == jnp.arange(latitudes, dtype=jnp.int32)[None, :]
    leaving = jnp.einsum(
        "rl,fstl->rtfs",
        onehot.astype(jnp.bfloat16),
        coefficients,
        preferred_element_type=jnp.float32,
    ).astype(jnp.bfloat16)
    leaving = jnp.pad(leaving, ((0, 0), (0, 0), (0, 0), (0, LANES - slot_count)))
    chunk_rows = own_rows * parts * own_fields
    leaving = leaving.reshape(devices, chunk_rows, LANES)
    places = np.arange(lanes * chunk_rows).reshape(lanes, own_rows, parts, own_fields)
    places = places.transpose(2, 1, 0, 3).reshape(-1)
    order = jnp.asarray(
        places[:, None] == np.arange(lanes * chunk_rows)[None, :], dtype=jnp.bfloat16
    )
    blocks, returned = round_trip(
        cycle_length,
        row_latitude,
        order,
        pair_band,
        leaving,
        gridpoint_factor,
        bands,
        lanes,
        fields,
    )
    grid_rows = blocks.reshape(lanes * own_rows, fields, points)[:band_rows]
    grid_rows = jnp.transpose(grid_rows, (1, 0, 2))
    returned = returned.reshape(devices * own_rows, parts, own_fields, LANES)
    back = onehot & inside[:, None]
    tendencies = jnp.einsum(
        "rtfs,rl->fstl",
        returned[..., :slot_count],
        back.astype(jnp.bfloat16),
        preferred_element_type=jnp.float32,
    ).astype(jnp.bfloat16)
    return (grid_rows, tendencies)


def solution(mesh):
    return jax.shard_map(
        on_device,
        mesh=mesh,
        in_specs=(P("lon", "band", None, None), P(), P(), P(), P("band", "lon")),
        out_specs=(P(None, "band", "lon"), P("lon", "band", None, None)),
        check_vma=False,
    )
```
